32 devices in a mesh: expert: 8 (over z, y), etp: 4 (over x, core).
Axes of the slice: x: 2, y: 2, z: 4, core: 2. Of those that a mesh axis runs over, the one named last changes fastest.
Arguments:
- tokens: bfloat16 [4096, 2560], P(('expert', 'etp')), may hold values from -6 to 6
- hidden_grad: bfloat16 [4096, 4096], P(('expert', 'etp')), may hold values from -6 to 6
- routes: int32 [4096, 1], P(('expert', 'etp')), may hold values from 0 to 7; in each aligned block of 512 rows (0 to 511, 512 to 1023, ...) at most 80 rows name the same one
- exponents: int32 [4096], P(('expert', 'etp')), may hold values from -2 to 2
- gate_weight: bfloat16 [8, 2560, 4096], P('expert', None, 'etp'), may hold values from -0.125 to 0.125
- up_weight: bfloat16 [8, 2560, 4096], P('expert', None, 'etp'), may hold values from -0.125 to 0.125
Outputs:
- input_grad: bfloat16 [4096, 2560], P(('expert', 'etp'))
The draws below stay inside these ranges and needn't reach their ends.
Inputs may be any that keep to these rules, and one draw needn't show every extreme that they name: `routes`: in each aligned block of 512 rows (the tokens of one group of devices along etp) no expert is named by more than 80 rows, and in every draw some expert is named by exactly 80 rows of some block.
All inputs are finite; a program needn't handle non-finite values.
Results may differ from the reference program's by a relative error of at most 0.0095.
Values may be sent and summed in bfloat16 or wider, within the bound.
A program may use at most 128 MiB of HBM per device.

```python
import math
import jax
import jax.numpy as jnp
import numpy as np
from jax import lax

D = 2560
FF = 4096
TOK_DEV = 128
EXPERTS = 8
TOKENS = 4096
C = 80
N_EXPERT = 8
N_ETP = 4


def touch_ends(drawn, key, smallest, high):
    longest = drawn.shape.index(max(drawn.shape))
    spots = []
    for shift in (0, 1):
        where = [jax.random.randint(jax.random.fold_in(key, axis), (), 0, length) for axis, length in enumerate(drawn.shape)]
        where[longest] = (where[longest] + shift) % drawn.shape[longest]
        spots.append(tuple(where))
    return drawn.at[spots[0]].set(smallest).at[spots[1]].set(high)


def level_of(key, extent, shards, smallest, largest):
    def one(position, shards_of):
        draws = jax.random.uniform(jax.random.fold_in(jax.random.fold_in(key, 6), position), (shards_of,), jnp.float32, smallest / len(shards), largest / len(shards))
        return jnp.repeat(jnp.exp(draws), extent[position] // shards_of).reshape((-1,) + (1,) * (len(extent) - position - 1))

    level = one(*shards[0])
    for cut in shards[1:]:
        level = level * one(*cut)
    return level


def shared_out(rng, own, number, rows, number_of, top, most, slope):
    order = jax.random.permutation(rng, number_of)
    packed, ordinary = load_shares(number_of, rows * top, most, slope, True), load_shares(number_of, rows * top, most, slope, False)
    places = jnp.arange(number_of)

    def named(lengths, turn):
        used = int((lengths > 0).sum())
        fixed = max(1, used // 4)
        passed = fixed + (places - fixed + turn * (used - fixed)) % max(1, number_of - fixed)
        return jnp.zeros((number_of,), jnp.int32).at[order[jnp.where(places < fixed, places, passed)]].set(jnp.asarray(lengths, jnp.int32))

    lengths = jnp.where(number % 4 == 0, named(packed, number // 4), named(ordinary, number - number // 4 - 1))
    mixed = jax.random.permutation(jax.random.fold_in(own, 3), number_of)
    donor, taker = mixed[0:number_of // 2 * 2:2], mixed[1:number_of // 2 * 2:2]
    room = jnp.minimum(lengths[donor] - 1, most - lengths[taker]) // 2
    room = jnp.where((donor == order[0]) | (taker == order[0]) | (lengths[taker] == 0), 0, jnp.maximum(room, 0))
    passed = jax.random.randint(jax.random.fold_in(own, 4), (number_of // 2,), 0, 1 << 20) % (room + 1)
    lengths = lengths.at[donor].add(-passed).at[taker].add(passed)
    items = jnp.searchsorted(jnp.cumsum(lengths), jnp.arange(rows * top), side="right").astype(jnp.int32)
    grid = items.reshape(top, rows).T
    grid = grid[jax.random.permutation(jax.random.fold_in(own, 1), rows)]
    turn = jax.random.randint(jax.random.fold_in(own, 2), (rows, 1), 0, top)
    return jnp.take_along_axis(grid, (jnp.arange(top)[None, :] + turn) % top, axis=1)


def load_shares(count, total, bound, skew, full):
    loads = [(1 << 20) // math.isqrt(standing ** skew) + 1 for standing in range(1, count + 1)]
    largest = bound if full else min(bound, max(-(-total // count), total * loads[0] // sum(loads)))
    least = 1 if total - largest >= count - 1 else 0
    given, spare = [largest] + [least] * (count - 1), total - largest - least * (count - 1)
    while spare > 0:
        free = [i for i in range(1, count) if given[i] < largest] or [i for i in range(1, count) if given[i] < bound]
        whole, budget = sum([loads[i] for i in free]), spare
        for i in free:
            more = min(bound - given[i], max(1, budget * loads[i] // whole), spare)
            given[i] = given[i] + more
            spare = spare - more
    return np.array(given)


def scatter_about(own_key, dims, deviation, bound, shards=(), kind=jnp.bfloat16):
    level = level_of(own_key, dims, shards, -0.22, 0.18) if shards else 1.0
    values = jax.random.normal(own_key, dims, jnp.float32) * deviation * level
    return jnp.minimum(jnp.maximum(values, -bound), bound).astype(kind)


def setup_inputs(seed: int = 0) -> dict:
    splits = jax.random.split(jax.random.key(seed), 7)
    tokens = scatter_about(splits[0], (TOKENS, D), 1.0, 6.0, ((0, 32),))
    hidden_grad = scatter_about(splits[1], (TOKENS, FF), 1.0, 6.0, ((0, 32),))
    routes_keys = jax.random.split(jax.random.fold_in(splits[2], 1), TOKENS // (N_ETP * TOK_DEV))
    routes_turns = jax.random.permutation(jax.random.fold_in(splits[2], 3), TOKENS // (N_ETP * TOK_DEV))
    routes = jax.vmap(lambda own, number: shared_out(jax.random.fold_in(splits[2], 2), own, number, N_ETP * TOK_DEV, EXPERTS, 1, C, 2))(routes_keys, routes_turns).reshape((TOKENS, 1))
    exponents = touch_ends(jax.random.randint(splits[3], (TOKENS,), -2, 3), jax.random.fold_in(splits[3], 1), -2, 2).astype(jnp.int32)
    gate_weight = scatter_about(splits[4], (EXPERTS, D, FF), D ** -0.5, 0.125, ((0, 8), (2, 4)))
    up_weight = scatter_about(splits[5], (EXPERTS, D, FF), D ** -0.5, 0.125, ((0, 8), (2, 4)))
    return dict(tokens=tokens, hidden_grad=hidden_grad, routes=routes, exponents=exponents, gate_weight=gate_weight, up_weight=up_weight)


def reference(tokens, hidden_grad, routes, exponents, gate_weight, up_weight):
    route_flat = routes[:, 0]
    total = route_flat.shape[0]
    positions = jnp.arange(total, dtype=jnp.int32)
    sorted_ids = jnp.argsort(route_flat * total + positions, stable=True).astype(jnp.int32)
    onehot = (route_flat[:, None] == jnp.arange(EXPERTS, dtype=jnp.int32)[None, :]).astype(jnp.int32)
    counts = jnp.sum(onehot, axis=0).astype(jnp.int32)
    starts = (jnp.cumsum(counts) - counts).astype(jnp.int32)
    slot_limit = N_EXPERT * C
    slot_range = jnp.arange(slot_limit, dtype=jnp.int32)
    scales = jnp.exp2(exponents.astype(jnp.float32))
    quarter = FF // N_ETP

    def per_expert(items):
        w_gate, w_up, row_count, first_row = items
        picked = sorted_ids[jnp.clip(first_row + slot_range, 0, total - 1)]
        live_slot = slot_range < row_count
        picked_rows = tokens[picked]
        scaled_grad = hidden_grad[picked].astype(jnp.float32) * scales[picked][:, None]
        gate_pre = jnp.dot(picked_rows, w_gate, preferred_element_type=jnp.float32)
        up_pre = jnp.dot(picked_rows, w_up, preferred_element_type=jnp.float32)
        sigmoid_gate = jax.nn.sigmoid(gate_pre)
        grad_gate = (scaled_grad * up_pre * sigmoid_gate * (1.0 + gate_pre * (1.0 - sigmoid_gate))).astype(jnp.bfloat16)
        grad_up = (scaled_grad * gate_pre * sigmoid_gate).astype(jnp.bfloat16)
        gate_split = grad_gate.astype(jnp.float32).reshape(slot_limit, N_ETP, quarter)
        up_split = grad_up.astype(jnp.float32).reshape(slot_limit, N_ETP, quarter)
        weight_gate = w_gate.astype(jnp.float32).reshape(D, N_ETP, quarter)
        weight_up = w_up.astype(jnp.float32).reshape(D, N_ETP, quarter)
        partial_value = jnp.einsum("mqf,dqf->qmd", gate_split, weight_gate) + jnp.einsum("mqf,dqf->qmd", up_split, weight_up)
        rounded = lax.optimization_barrier(partial_value.astype(jnp.bfloat16))
        summed = jnp.sum(rounded.astype(jnp.float32), axis=0).astype(jnp.bfloat16)
        target = jnp.where(live_slot, picked, total).astype(jnp.int32)
        return summed, target

    outputs, targets = lax.map(per_expert, (gate_weight, up_weight, counts, starts))
    result = jnp.zeros((total + 1, D), jnp.bfloat16).at[targets.reshape(-1)].set(outputs.reshape(-1, D))
    return result[:total]
```

```python
import functools

import jax
import jax.numpy as jnp
from jax import lax
from jax.experimental import pallas as pl
from jax.experimental.pallas import tpu as pltpu
from jax.sharding import PartitionSpec as P

MESH = pl.DeviceIdType.MESH
BF = jnp.bfloat16
F32 = jnp.float32


def flip(index, k, size):
    total, bit = 0, 1
    while bit < size:
        if (k // bit) % 2:
            total = total + bit * (1 - lax.rem(lax.div(index, bit), 2))
        else:
            total = total + bit * lax.rem(lax.div(index, bit), 2)
        bit *= 2
    return total


def quarter_of(p):
    return lax.rem(p, 2) * 2 + lax.div(p, 2)


def aligned(start, size, step=128):
    return pl.ds(pl.multiple_of(start, step), size)


def kernel(
    NE, NP, C, cap,
    meta, tok, hid, wg_hbm, wu_hbm, out,
    meta_rx, tok_rx, hid_rx, pm, pack_t, pack_h, full_t, arr_h, wg, wu, gg, gu,
    cs, ck, crx, xs, xrx, zs, ret, fs,
    loc, m_s, m_r, t_s, t_r, h_s, h_r, zt_s, zt_r, zh_s, zh_r, ag_s, ag_r,
    c_s, c_r, x_s, x_r, r_s, r_r, f_s, f_r,
):
    me_e, me_p = lax.axis_index("expert"), lax.axis_index("etp")
    B = NE // C
    M = B * cap
    T, D = tok.shape
    FL = wg.shape[1]
    Q, H = D // 4, D // 2
    TN = 256
    group = NP * T
    peers = [flip(me_p, j, NP) for j in range(NP)]
    far = [flip(me_e, k, NE) for k in range(NE)]
    my_cols = aligned(quarter_of(me_p) * Q, Q)

    def remote(src, dst, ss, rs, e, p):
        return pltpu.make_async_remote_copy(
            src_ref=src, dst_ref=dst, send_sem=ss, recv_sem=rs, device_id=(e, p), device_id_type=MESH
        )

    own_t = pltpu.make_async_copy(tok.at[:, my_cols], tok_rx.at[me_p], loc.at[0])
    own_h = pltpu.make_async_copy(hid.at[:, aligned(me_p * FL, FL)], hid_rx.at[me_p], loc.at[1])
    own_g = pltpu.make_async_copy(wg_hbm.at[0], wg, loc.at[2])
    own_u = pltpu.make_async_copy(wu_hbm.at[0], wu, loc.at[3])
    barrier = pltpu.get_barrier_semaphore()
    for j in range(1, NP):
        pl.semaphore_signal(barrier, inc=1, device_id=(me_e, peers[j]), device_id_type=MESH)
    for k in range(1, NE):
        pl.semaphore_signal(barrier, inc=1, device_id=(far[k], me_p), device_id_type=MESH)
    own_t.start()
    own_h.start()
    meta_rx[me_p] = meta[...]
    pl.semaphore_wait(barrier, NP - 1 + NE - 1)

    order = [2, 3, 1]
    started = []

    def go(copy):
        copy.start()
        started.append(copy)
        return copy

    metas = [go(remote(meta, meta_rx.at[me_p], m_s.at[j], m_r.at[j], me_e, peers[j])) for j in order]
    toks = [
        go(remote(tok.at[:, aligned(quarter_of(peers[j]) * Q, Q)], tok_rx.at[me_p], t_s.at[j], t_r.at[j], me_e, peers[j]))
        for j in order
    ]
    hids = [
        go(remote(hid.at[:, aligned(peers[j] * FL, FL)], hid_rx.at[me_p], h_s.at[j], h_r.at[j], me_e, peers[j]))
        for j in order
    ]
    own_g.start()
    own_u.start()

    for copy in metas:
        copy.wait_recv()
    route = jnp.concatenate([meta_rx[p][0:1, :] for p in range(NP)], axis=1)
    expo = jnp.concatenate([meta_rx[p][1:2, :] for p in range(NP)], axis=1)
    ids = lax.broadcasted_iota(jnp.int32, (NE, group), 0)
    onehot = jnp.where(ids == route, 1.0, 0.0)
    before = lax.broadcasted_iota(jnp.int32, (group, group), 0) <= lax.broadcasted_iota(jnp.int32, (group, group), 1)
    count = jnp.dot(onehot.astype(BF), jnp.where(before, 1.0, 0.0).astype(BF), preferred_element_type=F32)
    slot = jnp.sum(onehot * (ids.astype(F32) * cap + count - 1.0), axis=0, keepdims=True).astype(jnp.int32)
    scale = sum(jnp.where(expo == v, 2.0**v, 0.0) for v in range(-2, 3))
    rows = lax.broadcasted_iota(jnp.int32, (cap, group), 0)
    for c in range(C):
        for i in range(B):
            hit = jnp.where(rows + far[c * B + i] * cap == slot, 1.0, 0.0)
            pm[c, i * cap : (i + 1) * cap, :] = hit.astype(BF)

    own_t.wait()
    for copy in toks:
        copy.wait_recv()
    zts, zhs, rets = {}, {}, {}
    for c in range(C):
        block = jnp.dot(pm[c], tok_rx[...].reshape(group, Q), preferred_element_type=F32).astype(BF)
        pack_t[c] = block
        if c == 0:
            full_t[0, 0:cap, my_cols] = block[0:cap]
        for i in range(B):
            k = c * B + i
            if k:
                r = pl.ds(i * cap, cap)
                zts[k] = go(remote(pack_t.at[c, r], full_t.at[c, r, my_cols], zt_s.at[k], zt_r.at[k], far[k], me_p))
    own_h.wait()
    for copy in hids:
        copy.wait_recv()
    for c in range(C):
        scaled = (pm[c].astype(F32) * scale).astype(BF)
        block = jnp.dot(scaled, hid_rx[...].reshape(group, FL), preferred_element_type=F32).astype(BF)
        pack_h[c] = block
        if c == 0:
            arr_h[0, 0:cap, :] = block[0:cap]
        for i in range(B):
            k = c * B + i
            if k:
                r = pl.ds(i * cap, cap)
                zhs[k] = go(remote(pack_h.at[c, r], arr_h.at[c, r], zh_s.at[k], zh_r.at[k], far[k], me_p))

    their_cols = aligned(quarter_of(peers[2]) * Q, Q)
    spread = {}

    def share(c):
        for k in range(max(1, c * B), (c + 1) * B):
            zts[k].wait_recv()
        part = full_t.at[c, :, my_cols]
        spread[1, c] = go(remote(part, part, ag_s.at[1, c], ag_r.at[1, c], me_e, peers[2]))
        spread[0, c] = go(remote(part, part, ag_s.at[0, c], ag_r.at[0, c], me_e, peers[1]))

    def forward(c):
        spread[1, c].wait_recv()
        part = full_t.at[c, :, their_cols]
        spread[2, c] = go(remote(part, part, ag_s.at[2, c], ag_r.at[2, c], me_e, peers[1]))

    half = lax.rem(me_p, 2)
    side = lax.div(me_p, 2)
    nt = (((1,), (1,)), ((), ()))
    crossed, sided = {}, {}

    def compute(c):
        spread[0, c].wait_recv()
        spread[2, c].wait_recv()
        for k in range(max(1, c * B), (c + 1) * B):
            zhs[k].wait_recv()

        def first(n, carry):
            cols = aligned(n * TN, TN)
            x = full_t[c]
            gate = jnp.dot(x, wg[:, cols], preferred_element_type=F32)
            up = jnp.dot(x, wu[:, cols], preferred_element_type=F32)
            grad = arr_h[c, :, cols].astype(F32)
            s = 1.0 / (1.0 + jnp.exp(-gate))
            gg[:, cols] = (grad * up * s * (1.0 + gate * (1.0 - s))).astype(BF)
            gu[:, cols] = (grad * gate * s).astype(BF)
            return carry

        lax.fori_loop(0, FL // TN, first, 0)

        def back(start):
            r = aligned(start, TN)
            return lax.dot_general(gg[...], wg[r, :], nt, preferred_element_type=F32) + lax.dot_general(
                gu[...], wu[r, :], nt, preferred_element_type=F32
            )

        def give(t, carry):
            cs[c, :, aligned(t * TN, TN)] = back((1 - half) * H + t * TN).astype(BF)
            return carry

        def keep(t, carry):
            ck[c, :, aligned(t * TN, TN)] = back(half * H + t * TN)
            return carry

        lax.fori_loop(0, H // TN, give, 0)
        crossed[c] = go(remote(cs.at[c], crx.at[c], c_s.at[c], c_r.at[c], me_e, peers[1]))
        lax.fori_loop(0, H // TN, keep, 0)

    def x_step(c):
        crossed[c].wait_recv()
        cols = aligned((1 - side) * Q, Q)
        xs[c] = (ck[c, :, cols] + crx[c, :, cols].astype(F32)).astype(BF)
        sided[c] = go(remote(xs.at[c], xrx.at[c], x_s.at[c], x_r.at[c], me_e, peers[2]))

    def z_step(c):
        sided[c].wait_recv()
        cols = aligned(side * Q, Q)
        total = (ck[c, :, cols] + crx[c, :, cols].astype(F32) + xrx[c].astype(F32)).astype(BF)
        zs[c] = total
        if c == 0:
            ret[0, 0:cap, :] = total[0:cap]
        for i in range(B):
            k = c * B + i
            if k:
                r = pl.ds(i * cap, cap)
                rets[k] = go(remote(zs.at[c, r], ret.at[c, r], r_s.at[k], r_r.at[k], far[k], me_p))

    share(0)
    forward(0)
    if C > 1:
        share(1)
        forward(1)
    own_g.wait()
    own_u.wait()
    for c in range(C):
        if 0 < c < C - 1:
            share(c + 1)
            forward(c + 1)
        compute(c)
        if c >= 1:
            x_step(c - 1)
        if c >= 2:
            z_step(c - 2)
    x_step(C - 1)
    if C > 1:
        z_step(C - 2)
    z_step(C - 1)

    for k in range(1, NE):
        rets[k].wait_recv()
    tn = (((0,), (0,)), ((), ()))
    ends = []
    for j in order + [0]:
        cols = aligned(peers[j] * T, T)
        rows_j = sum(
            lax.dot_general(pm[c, :, cols], ret[c], tn, preferred_element_type=F32) for c in range(C)
        ).astype(BF)
        if j:
            fs[j] = rows_j
            ends.append(go(remote(fs.at[j], out.at[:, my_cols], f_s.at[j], f_r.at[j], me_e, peers[j])))
        else:
            out[:, my_cols] = rows_j
    for copy in ends:
        copy.wait_recv()
    for copy in started:
        copy.wait_send()


def on_device(NE, NP, tokens, hidden_grad, routes, exponents, gate_weight, up_weight):
    T, D = tokens.shape
    FL = gate_weight.shape[2]
    group = NP * T
    experts = NE * gate_weight.shape[0]
    cap = -(-max(2, 5 * group // (4 * experts)) // 16) * 16
    C = min(4, NE)
    M = NE // C * cap
    Q, H = D // 4, D // 2
    meta = jnp.concatenate(
        [routes[:, 0][None, :], exponents[None, :], jnp.zeros((6, T), jnp.int32)], axis=0
    )
    V = pltpu.VMEM
    dma = pltpu.SemaphoreType.DMA
    return pl.pallas_call(
        functools.partial(kernel, NE, NP, C, cap),
        out_shape=jax.ShapeDtypeStruct((T, D), BF),
        in_specs=[pl.BlockSpec(memory_space=V)] + [pl.BlockSpec(memory_space=pl.ANY)] * 4,
        out_specs=pl.BlockSpec(memory_space=V),
        scratch_shapes=[
            V((NP, 8, T), jnp.int32),
            V((NP, T, Q), BF),
            V((NP, T, FL), BF),
            V((C, M, group), BF),
            V((C, M, Q), BF),
            V((C, M, FL), BF),
            V((C, M, D), BF),
            V((C, M, FL), BF),
            V((D, FL), BF),
            V((D, FL), BF),
            V((M, FL), BF),
            V((M, FL), BF),
            V((C, M, H), BF),
            V((C, M, H), F32),
            V((C, M, H), BF),
            V((C, M, Q), BF),
            V((C, M, Q), BF),
            V((C, M, Q), BF),
            V((C, M, Q), BF),
            V((NP, T, Q), BF),
            dma((4,)),
            dma((NP,)), dma((NP,)), dma((NP,)), dma((NP,)), dma((NP,)), dma((NP,)),
            dma((NE,)), dma((NE,)), dma((NE,)), dma((NE,)),
            dma((3, C)), dma((3, C)),
            dma((C,)), dma((C,)), dma((C,)), dma((C,)),
            dma((NE,)), dma((NE,)),
            dma((NP,)), dma((NP,)),
        ],
        compiler_params=pltpu.CompilerParams(
            collective_id=0, has_side_effects=True, vmem_limit_bytes=60 * 1024 * 1024
        ),
    )(meta, tokens, hidden_grad, gate_weight, up_weight)


def solution(mesh):
    placed = (
        P(("expert", "etp"), None),
        P(("expert", "etp"), None),
        P(("expert", "etp"), None),
        P(("expert", "etp")),
        P("expert", None, "etp"),
        P("expert", None, "etp"),
    )
    body = functools.partial(on_device, mesh.shape["expert"], mesh.shape["etp"])
    return jax.shard_map(
        body, mesh=mesh, in_specs=placed, out_specs=P(("expert", "etp"), None), check_vma=False
    )
```

```python
import functools

import jax
import jax.numpy as jnp
from jax import lax
from jax.experimental import pallas as pl
from jax.experimental.pallas import tpu as pltpu
from jax.sharding import PartitionSpec as P

MESH = pl.DeviceIdType.MESH
BF = jnp.bfloat16
F32 = jnp.float32


def flip(index, k, size):
    total, bit = 0, 1
    while bit < size:
        if (k // bit) % 2:
            total = total + bit * (1 - lax.rem(lax.div(index, bit), 2))
        else:
            total = total + bit * lax.rem(lax.div(index, bit), 2)
        bit *= 2
    return total


def quarter_of(p):
    return lax.rem(p, 2) * 2 + lax.div(p, 2)


def aligned(start, size, step=128):
    return pl.ds(pl.multiple_of(start, step), size)


def kernel(
    NE, NP, C, cap,
    routes, expos, tok, hid, wg_hbm, wu_hbm, out,
    route_rx, expo_rx, tok_rx, hid_rx, pm, pack_t, pack_h, full_t, arr_h, wg, wu, gate_s, up_s, gg, gu,
    cs, ck, crx, xs, xrx, zs, ret, fs,
    loc, m_s, m_r, e_s, e_r, t_s, t_r, h_s, h_r, zt_s, zt_r, zh_s, zh_r, ag_s, ag_r,
    c_s, c_r, x_s, x_r, r_s, r_r, f_s, f_r,
):
    me_e, me_p = lax.axis_index("expert"), lax.axis_index("etp")
    B = NE // C
    M = B * cap
    T, D = tok.shape
    FL = wg.shape[1]
    Q, H = D // 4, D // 2
    TN = 256
    group = NP * T
    cut = max(128, Q // 256 * 128)
    pieces = [(0, cut), (cut, Q - cut)]
    peers = [flip(me_p, j, NP) for j in range(NP)]
    far = [flip(me_e, k, NE) for k in range(NE)]
    my_base = quarter_of(me_p) * Q
    my_cols = aligned(my_base, Q)

    def remote(src, dst, ss, rs, e, p):
        return pltpu.make_async_remote_copy(
            src_ref=src, dst_ref=dst, send_sem=ss, recv_sem=rs, device_id=(e, p), device_id_type=MESH
        )

    own_t = pltpu.make_async_copy(tok.at[:, my_cols], tok_rx.at[me_p], loc.at[0])
    own_h = pltpu.make_async_copy(hid.at[:, aligned(me_p * FL, FL)], hid_rx.at[me_p], loc.at[1])
    own_g = pltpu.make_async_copy(wg_hbm.at[0], wg, loc.at[2])
    own_u = pltpu.make_async_copy(wu_hbm.at[0], wu, loc.at[3])
    barrier = pltpu.get_barrier_semaphore()
    for j in range(1, NP):
        pl.semaphore_signal(barrier, inc=1, device_id=(me_e, peers[j]), device_id_type=MESH)
    for k in range(1, NE):
        pl.semaphore_signal(barrier, inc=1, device_id=(far[k], me_p), device_id_type=MESH)
    own_t.start()
    own_h.start()
    route_rx[me_p] = routes[...]
    expo_rx[me_p] = expos[...]
    pl.semaphore_wait(barrier, NP - 1 + NE - 1)

    order = [2, 3, 1]
    started = []

    def go(copy):
        copy.start()
        started.append(copy)
        return copy

    metas = [go(remote(routes, route_rx.at[me_p], m_s.at[j], m_r.at[j], me_e, peers[j])) for j in order]
    metas += [go(remote(expos, expo_rx.at[me_p], e_s.at[j], e_r.at[j], me_e, peers[j])) for j in order]
    toks = [
        [
            go(remote(
                tok.at[:, aligned(quarter_of(peers[j]) * Q + lo, n)], tok_rx.at[me_p, :, pl.ds(lo, n)],
                t_s.at[s, j], t_r.at[s, j], me_e, peers[j],
            ))
            for j in order
        ]
        for s, (lo, n) in enumerate(pieces)
    ]
    hids = [
        go(remote(hid.at[:, aligned(peers[j] * FL, FL)], hid_rx.at[me_p], h_s.at[j], h_r.at[j], me_e, peers[j]))
        for j in order
    ]
    own_g.start()
    own_u.start()

    for copy in metas:
        copy.wait_recv()
    route = jnp.concatenate([route_rx[p] for p in range(NP)], axis=1)
    expo = jnp.concatenate([expo_rx[p] for p in range(NP)], axis=1)
    ids = lax.broadcasted_iota(jnp.int32, (NE, group), 0)
    onehot = jnp.where(ids == route, 1.0, 0.0)
    before = lax.broadcasted_iota(jnp.int32, (group, group), 0) <= lax.broadcasted_iota(jnp.int32, (group, group), 1)
    count = jnp.dot(onehot.astype(BF), jnp.where(before, 1.0, 0.0).astype(BF), preferred_element_type=F32)
    slot = jnp.sum(onehot * (ids.astype(F32) * cap + count - 1.0), axis=0, keepdims=True).astype(jnp.int32)
    scale = sum(jnp.where(expo == v, 2.0**v, 0.0) for v in range(-2, 3))
    rows = lax.broadcasted_iota(jnp.int32, (cap, group), 0)
    for c in range(C):
        for i in range(B):
            hit = jnp.where(rows + far[c * B + i] * cap == slot, 1.0, 0.0)
            pm[c, i * cap : (i + 1) * cap, :] = hit.astype(BF)

    own_t.wait()
    zts, zhs, rets = {}, {}, {}
    for s, (lo, n) in enumerate(pieces):
        for copy in toks[s]:
            copy.wait_recv()
        for c in range(C):
            piece = tok_rx[:, :, lo : lo + n].reshape(group, n)
            block = jnp.dot(pm[c], piece, preferred_element_type=F32).astype(BF)
            pack_t[c, :, lo : lo + n] = block
            cols = aligned(my_base + lo, n)
            if c == 0:
                full_t[0, 0:cap, cols] = block[0:cap]
            for i in range(B):
                k = c * B + i
                if k:
                    r = pl.ds(i * cap, cap)
                    zts[k, s] = go(remote(
                        pack_t.at[c, r, pl.ds(lo, n)], full_t.at[c, r, cols], zt_s.at[s, k], zt_r.at[s, k], far[k], me_p
                    ))
    own_h.wait()
    for copy in hids:
        copy.wait_recv()
    for c in ([2, 3, 0, 1] if C == 4 else range(C)):
        scaled = (pm[c].astype(F32) * scale).astype(BF)
        block = jnp.dot(scaled, hid_rx[...].reshape(group, FL), preferred_element_type=F32).astype(BF)
        pack_h[c] = block
        if c == 0:
            arr_h[0, 0:cap, :] = block[0:cap]
        for i in range(B):
            k = c * B + i
            if k:
                r = pl.ds(i * cap, cap)
                zhs[k] = go(remote(pack_h.at[c, r], arr_h.at[c, r], zh_s.at[k], zh_r.at[k], far[k], me_p))

    their_cols = aligned(quarter_of(peers[2]) * Q, Q)
    spread = {}

    def share(c):
        for k in range(max(1, c * B), (c + 1) * B):
            zts[k, 0].wait_recv()
            zts[k, 1].wait_recv()
        part = full_t.at[c, :, my_cols]
        spread[1, c] = go(remote(part, part, ag_s.at[1, c], ag_r.at[1, c], me_e, peers[2]))
        spread[0, c] = go(remote(part, part, ag_s.at[0, c], ag_r.at[0, c], me_e, peers[1]))

    def forward(c):
        spread[1, c].wait_recv()
        part = full_t.at[c, :, their_cols]
        spread[2, c] = go(remote(part, part, ag_s.at[2, c], ag_r.at[2, c], me_e, peers[1]))

    half = lax.rem(me_p, 2)
    side = lax.div(me_p, 2)
    nt = (((1,), (1,)), ((), ()))
    crossed, sided = {}, {}
    tiles = H // TN
    lead = -(-Q // TN)
    sent_q, kept_q = (1 - side) * Q, side * Q

    def tile_at(t):
        return (side * t + (1 - side) * (tiles - 1 - t)) * TN

    def forth(c):
        spread[0, c].wait_recv()
        spread[2, c].wait_recv()

        def step(n, carry):
            cols = aligned(n * TN, TN)
            x = full_t[c]
            gate_s[c, :, cols] = jnp.dot(x, wg[:, cols], preferred_element_type=F32)
            up_s[c, :, cols] = jnp.dot(x, wu[:, cols], preferred_element_type=F32)
            return carry

        lax.fori_loop(0, FL // TN, step, 0)

    def back(c, between=None):
        for k in range(max(1, c * B), (c + 1) * B):
            zhs[k].wait_recv()

        def act(n, carry):
            cols = aligned(n * TN, TN)
            gate, up = gate_s[c, :, cols], up_s[c, :, cols]
            grad = arr_h[c, :, cols].astype(F32)
            s = 1.0 / (1.0 + jnp.exp(-gate))
            gg[:, cols] = (grad * up * s * (1.0 + gate * (1.0 - s))).astype(BF)
            gu[:, cols] = (grad * gate * s).astype(BF)
            return carry

        lax.fori_loop(0, FL // TN, act, 0)

        def product(start):
            r = aligned(start, TN)
            return lax.dot_general(gg[...], wg[r, :], nt, preferred_element_type=F32) + lax.dot_general(
                gu[...], wu[r, :], nt, preferred_element_type=F32
            )

        def give(t, carry):
            cs[c, :, aligned(tile_at(t), TN)] = product((1 - half) * H + tile_at(t)).astype(BF)
            return carry

        def keep(t, carry):
            ck[c, :, aligned(tile_at(t), TN)] = product(half * H + tile_at(t))
            return carry

        def cross(q, base):
            part = pl.ds(pl.multiple_of(base, 128), Q)
            crossed[q, c] = go(remote(
                cs.at[c, :, part], crx.at[c, :, part], c_s.at[q, c], c_r.at[q, c], me_e, peers[1]
            ))

        lax.fori_loop(0, lead, give, 0)
        cross(0, sent_q)
        lax.fori_loop(lead, tiles, give, 0)
        cross(1, kept_q)
        lax.fori_loop(0, lead, keep, 0)
        crossed[0, c].wait_recv()
        for s, (lo, n) in enumerate(pieces):
            cols = aligned(sent_q + lo, n)
            here = pl.ds(lo, n)
            xs[c, :, here] = (ck[c, :, cols] + crx[c, :, cols].astype(F32)).astype(BF)
            sided[s, c] = go(remote(
                xs.at[c, :, here], xrx.at[c, :, here], x_s.at[s, c], x_r.at[s, c], me_e, peers[2]
            ))
        if between is not None:
            between()
        lax.fori_loop(lead, tiles, keep, 0)

    def z_step(c):
        crossed[1, c].wait_recv()
        for s, (lo, n) in enumerate(pieces):
            sided[s, c].wait_recv()
            cols = aligned(kept_q + lo, n)
            here = pl.ds(lo, n)
            total = (ck[c, :, cols] + crx[c, :, cols].astype(F32) + xrx[c, :, here].astype(F32)).astype(BF)
            zs[c, :, here] = total
            if c == 0:
                ret[0, 0:cap, here] = total[0:cap]
            for i in range(B):
                k = c * B + i
                if k:
                    r = pl.ds(i * cap, cap)
                    rets[k, s] = go(remote(
                        zs.at[c, r, here], ret.at[c, r, here], r_s.at[s, k], r_r.at[s, k], far[k], me_p
                    ))

    def gather(c):
        share(c)
        forward(c)

    if C == 4:
        gather(0)
        gather(1)
        own_g.wait()
        own_u.wait()
        forth(0)
        gather(2)
        forth(1)
        gather(3)
        forth(2)
        forth(3)
        back(2)
        back(0)
        z_step(2)
        back(3)
        z_step(0)
        back(1, lambda: z_step(3))
        z_step(1)
    else:
        own_g.wait()
        own_u.wait()
        for c in range(C):
            gather(c)
            forth(c)
            back(c)
            z_step(c)

    tn = (((0,), (0,)), ((), ()))
    ends = []
    for s, (lo, n) in enumerate(pieces):
        for k in range(1, NE):
            rets[k, s].wait_recv()
        here = pl.ds(lo, n)
        cols = aligned(my_base + lo, n)
        piece = ret[:, :, lo : lo + n].reshape(C * M, n)
        for j in order + [0]:
            pick = pm[:, :, aligned(peers[j] * T, T)].reshape(C * M, T)
            rows_j = lax.dot_general(pick, piece, tn, preferred_element_type=F32).astype(BF)
            if j:
                fs[j, :, here] = rows_j
                ends.append(go(remote(fs.at[j, :, here], out.at[:, cols], f_s.at[s, j], f_r.at[s, j], me_e, peers[j])))
            else:
                out[:, cols] = rows_j
    for copy in ends:
        copy.wait_recv()
    for copy in started:
        copy.wait_send()


def on_device(NE, NP, tokens, hidden_grad, routes, exponents, gate_weight, up_weight):
    T, D = tokens.shape
    FL = gate_weight.shape[2]
    group = NP * T
    experts = NE * gate_weight.shape[0]
    cap = -(-max(2, 5 * group // (4 * experts)) // 16) * 16
    C = min(4, NE)
    M = NE // C * cap
    Q, H = D // 4, D // 2
    V = pltpu.VMEM
    dma = pltpu.SemaphoreType.DMA
    return pl.pallas_call(
        functools.partial(kernel, NE, NP, C, cap),
        out_shape=jax.ShapeDtypeStruct((T, D), BF),
        in_specs=[pl.BlockSpec(memory_space=V)] * 2 + [pl.BlockSpec(memory_space=pl.ANY)] * 4,
        out_specs=pl.BlockSpec(memory_space=V),
        scratch_shapes=[
            V((NP, 1, T), jnp.int32),
            V((NP, 1, T), jnp.int32),
            V((NP, T, Q), BF),
            V((NP, T, FL), BF),
            V((C, M, group), BF),
            V((C, M, Q), BF),
            V((C, M, FL), BF),
            V((C, M, D), BF),
            V((C, M, FL), BF),
            V((D, FL), BF),
            V((D, FL), BF),
            V((C, M, FL), F32),
            V((C, M, FL), F32),
            V((M, FL), BF),
            V((M, FL), BF),
            V((C, M, H), BF),
            V((C, M, H), F32),
            V((C, M, H), BF),
            V((C, M, Q), BF),
            V((C, M, Q), BF),
            V((C, M, Q), BF),
            V((C, M, Q), BF),
            V((NP, T, Q), BF),
            dma((4,)),
            dma((NP,)), dma((NP,)), dma((NP,)), dma((NP,)),
            dma((2, NP)), dma((2, NP)), dma((NP,)), dma((NP,)),
            dma((2, NE)), dma((2, NE)), dma((NE,)), dma((NE,)),
            dma((3, C)), dma((3, C)),
            dma((2, C)), dma((2, C)), dma((2, C)), dma((2, C)),
            dma((2, NE)), dma((2, NE)),
            dma((2, NP)), dma((2, NP)),
        ],
        compiler_params=pltpu.CompilerParams(
            collective_id=0, has_side_effects=True, vmem_limit_bytes=60 * 1024 * 1024
        ),
    )(routes.reshape(1, T), exponents.reshape(1, T), tokens, hidden_grad, gate_weight, up_weight)


def solution(mesh):
    placed = (
        P(("expert", "etp"), None),
        P(("expert", "etp"), None),
        P(("expert", "etp"), None),
        P(("expert", "etp")),
        P("expert", None, "etp"),
        P("expert", None, "etp"),
    )
    body = functools.partial(on_device, mesh.shape["expert"], mesh.shape["etp"])
    return jax.shard_map(
        body, mesh=mesh, in_specs=placed, out_specs=P(("expert", "etp"), None), check_vma=False
    )
```

```python
import functools

import jax
import jax.numpy as jnp
from jax import lax
from jax.experimental import pallas as pl
from jax.experimental.pallas import tpu as pltpu
from jax.sharding import PartitionSpec as P

MESH = pl.DeviceIdType.MESH
BF = jnp.bfloat16
F32 = jnp.float32


def flip(index, k, size):
    total, bit = 0, 1
    while bit < size:
        if (k // bit) % 2:
            total = total + bit * (1 - lax.rem(lax.div(index, bit), 2))
        else:
            total = total + bit * lax.rem(lax.div(index, bit), 2)
        bit *= 2
    return total


def quarter_of(p):
    return lax.rem(p, 2) * 2 + lax.div(p, 2)


def aligned(start, size, step=128):
    return pl.ds(pl.multiple_of(start, step), size)


def kernel(
    NE, NP, C, cap,
    routes, expos, tok, hid, wg_hbm, wu_hbm, out,
    route_rx, expo_rx, tok_rx, hid_rx, pm, pack_t, pack_h, full_t, arr_h, wg, wu, wgt, wut, gate_s, up_s, gg, gu,
    cs, ck, crx, xs, xrx, zs, ret, fs,
    loc, m_s, m_r, e_s, e_r, t_s, t_r, h_s, h_r, zt_s, zt_r, zh_s, zh_r, ag_s, ag_r,
    c_s, c_r, x_s, x_r, r_s, r_r, f_s, f_r,
):
    me_e, me_p = lax.axis_index("expert"), lax.axis_index("etp")
    B = NE // C
    M = B * cap
    T, D = tok.shape
    FL = wg.shape[1]
    Q, H = D // 4, D // 2
    TN = 256
    group = NP * T
    cut = max(128, Q // 256 * 128)
    pieces = [(0, cut), (cut, Q - cut)]
    peers = [flip(me_p, j, NP) for j in range(NP)]
    far = [flip(me_e, k, NE) for k in range(NE)]
    my_base = quarter_of(me_p) * Q
    my_cols = aligned(my_base, Q)

    def remote(src, dst, ss, rs, e, p):
        return pltpu.make_async_remote_copy(
            src_ref=src, dst_ref=dst, send_sem=ss, recv_sem=rs, device_id=(e, p), device_id_type=MESH
        )

    own_t = pltpu.make_async_copy(tok.at[:, my_cols], tok_rx.at[me_p], loc.at[0])
    own_h = pltpu.make_async_copy(hid.at[:, aligned(me_p * FL, FL)], hid_rx.at[me_p], loc.at[1])
    own_g = pltpu.make_async_copy(wg_hbm.at[0], wg, loc.at[2])
    own_u = pltpu.make_async_copy(wu_hbm.at[0], wu, loc.at[3])
    barrier = pltpu.get_barrier_semaphore()
    for j in range(1, NP):
        pl.semaphore_signal(barrier, inc=1, device_id=(me_e, peers[j]), device_id_type=MESH)
    for k in range(1, NE):
        pl.semaphore_signal(barrier, inc=1, device_id=(far[k], me_p), device_id_type=MESH)
    own_t.start()
    own_h.start()
    route_rx[me_p] = routes[...]
    expo_rx[me_p] = expos[...]
    pl.semaphore_wait(barrier, NP - 1 + NE - 1)

    order = [2, 3, 1]
    started = []

    def go(copy):
        copy.start()
        started.append(copy)
        return copy

    metas = [go(remote(routes, route_rx.at[me_p], m_s.at[j], m_r.at[j], me_e, peers[j])) for j in order]
    metas += [go(remote(expos, expo_rx.at[me_p], e_s.at[j], e_r.at[j], me_e, peers[j])) for j in order]
    toks = [
        [
            go(remote(
                tok.at[:, aligned(quarter_of(peers[j]) * Q + lo, n)], tok_rx.at[me_p, :, pl.ds(lo, n)],
                t_s.at[s, j], t_r.at[s, j], me_e, peers[j],
            ))
            for j in order
        ]
        for s, (lo, n) in enumerate(pieces)
    ]
    hids = [
        go(remote(hid.at[:, aligned(peers[j] * FL, FL)], hid_rx.at[me_p], h_s.at[j], h_r.at[j], me_e, peers[j]))
        for j in order
    ]
    own_g.start()
    own_u.start()

    for copy in metas:
        copy.wait_recv()
    route = jnp.concatenate([route_rx[p] for p in range(NP)], axis=1)
    expo = jnp.concatenate([expo_rx[p] for p in range(NP)], axis=1)
    ids = lax.broadcasted_iota(jnp.int32, (NE, group), 0)
    onehot = jnp.where(ids == route, 1.0, 0.0)
    before = lax.broadcasted_iota(jnp.int32, (group, group), 0) <= lax.broadcasted_iota(jnp.int32, (group, group), 1)
    count = jnp.dot(onehot.astype(BF), jnp.where(before, 1.0, 0.0).astype(BF), preferred_element_type=F32)
    slot = jnp.sum(onehot * (ids.astype(F32) * cap + count - 1.0), axis=0, keepdims=True).astype(jnp.int32)
    scale = sum(jnp.where(expo == v, 2.0**v, 0.0) for v in range(-2, 3))
    rows = lax.broadcasted_iota(jnp.int32, (cap, group), 0)
    for c in range(C):
        for i in range(B):
            hit = jnp.where(rows + far[c * B + i] * cap == slot, 1.0, 0.0)
            pm[c, i * cap : (i + 1) * cap, :] = hit.astype(BF)

    own_t.wait()
    zts, zhs, rets = {}, {}, {}
    for s, (lo, n) in enumerate(pieces):
        for copy in toks[s]:
            copy.wait_recv()
        for c in range(C):
            piece = tok_rx[:, :, lo : lo + n].reshape(group, n)
            block = jnp.dot(pm[c], piece, preferred_element_type=F32).astype(BF)
            pack_t[c, :, lo : lo + n] = block
            cols = aligned(my_base + lo, n)
            if c == 0:
                full_t[0, 0:cap, cols] = block[0:cap]
            for i in range(B):
                k = c * B + i
                if k:
                    r = pl.ds(i * cap, cap)
                    zts[k, s] = go(remote(
                        pack_t.at[c, r, pl.ds(lo, n)], full_t.at[c, r, cols], zt_s.at[s, k], zt_r.at[s, k], far[k], me_p
                    ))
    own_g.wait()
    own_u.wait()

    def turn(n, carry):
        r = aligned(n * TN, TN)
        wgt[:, r] = wg[r, :].T
        wut[:, r] = wu[r, :].T
        return carry

    lax.fori_loop(0, D // TN, turn, 0)
    own_h.wait()
    for copy in hids:
        copy.wait_recv()
    for c in ([2, 3, 0, 1] if C == 4 else range(C)):
        scaled = (pm[c].astype(F32) * scale).astype(BF)
        block = jnp.dot(scaled, hid_rx[...].reshape(group, FL), preferred_element_type=F32).astype(BF)
        pack_h[c] = block
        if c == 0:
            arr_h[0, 0:cap, :] = block[0:cap]
        for i in range(B):
            k = c * B + i
            if k:
                r = pl.ds(i * cap, cap)
                zhs[k] = go(remote(pack_h.at[c, r], arr_h.at[c, r], zh_s.at[k], zh_r.at[k], far[k], me_p))

    their_cols = aligned(quarter_of(peers[2]) * Q, Q)
    spread = {}

    def share(c):
        for k in range(max(1, c * B), (c + 1) * B):
            zts[k, 0].wait_recv()
            zts[k, 1].wait_recv()
        part = full_t.at[c, :, my_cols]
        spread[1, c] = go(remote(part, part, ag_s.at[1, c], ag_r.at[1, c], me_e, peers[2]))
        spread[0, c] = go(remote(part, part, ag_s.at[0, c], ag_r.at[0, c], me_e, peers[1]))

    def forward(c):
        spread[1, c].wait_recv()
        part = full_t.at[c, :, their_cols]
        spread[2, c] = go(remote(part, part, ag_s.at[2, c], ag_r.at[2, c], me_e, peers[1]))

    half = lax.rem(me_p, 2)
    side = lax.div(me_p, 2)
    crossed, sided = {}, {}
    tiles = H // TN
    lead = -(-Q // TN)
    sent_q, kept_q = (1 - side) * Q, side * Q

    def tile_at(t):
        return (side * t + (1 - side) * (tiles - 1 - t)) * TN

    def forth(c):
        spread[0, c].wait_recv()
        spread[2, c].wait_recv()

        def step(n, carry):
            cols = aligned(n * TN, TN)
            x = full_t[c]
            gate_s[c, :, cols] = jnp.dot(x, wg[:, cols], preferred_element_type=F32)
            up_s[c, :, cols] = jnp.dot(x, wu[:, cols], preferred_element_type=F32)
            return carry

        lax.fori_loop(0, FL // TN, step, 0)

    def back(c, between=None):
        for k in range(max(1, c * B), (c + 1) * B):
            zhs[k].wait_recv()

        def act(n, carry):
            cols = aligned(n * TN, TN)
            gate, up = gate_s[c, :, cols], up_s[c, :, cols]
            grad = arr_h[c, :, cols].astype(F32)
            s = 1.0 / (1.0 + jnp.exp(-gate))
            gg[:, cols] = (grad * up * s * (1.0 + gate * (1.0 - s))).astype(BF)
            gu[:, cols] = (grad * gate * s).astype(BF)
            return carry

        lax.fori_loop(0, FL // TN, act, 0)

        def product(start):
            r = aligned(start, TN)
            return jnp.dot(gg[...], wgt[:, r], preferred_element_type=F32) + jnp.dot(
                gu[...], wut[:, r], preferred_element_type=F32
            )

        def give(t, carry):
            cs[c, :, aligned(tile_at(t), TN)] = product((1 - half) * H + tile_at(t)).astype(BF)
            return carry

        def keep(t, carry):
            ck[c, :, aligned(tile_at(t), TN)] = product(half * H + tile_at(t))
            return carry

        def cross(q, base):
            part = pl.ds(pl.multiple_of(base, 128), Q)
            crossed[q, c] = go(remote(
                cs.at[c, :, part], crx.at[c, :, part], c_s.at[q, c], c_r.at[q, c], me_e, peers[1]
            ))

        lax.fori_loop(0, lead, give, 0)
        cross(0, sent_q)
        lax.fori_loop(lead, tiles, give, 0)
        cross(1, kept_q)
        lax.fori_loop(0, lead, keep, 0)
        crossed[0, c].wait_recv()
        for s, (lo, n) in enumerate(pieces):
            cols = aligned(sent_q + lo, n)
            here = pl.ds(lo, n)
            xs[c, :, here] = (ck[c, :, cols] + crx[c, :, cols].astype(F32)).astype(BF)
            sided[s, c] = go(remote(
                xs.at[c, :, here], xrx.at[c, :, here], x_s.at[s, c], x_r.at[s, c], me_e, peers[2]
            ))
        if between is not None:
            between()
        lax.fori_loop(lead, tiles, keep, 0)

    def z_step(c):
        crossed[1, c].wait_recv()
        for s, (lo, n) in enumerate(pieces):
            sided[s, c].wait_recv()
            cols = aligned(kept_q + lo, n)
            here = pl.ds(lo, n)
            total = (ck[c, :, cols] + crx[c, :, cols].astype(F32) + xrx[c, :, here].astype(F32)).astype(BF)
            zs[c, :, here] = total
            if c == 0:
                ret[0, 0:cap, here] = total[0:cap]
            for i in range(B):
                k = c * B + i
                if k:
                    r = pl.ds(i * cap, cap)
                    rets[k, s] = go(remote(
                        zs.at[c, r, here], ret.at[c, r, here], r_s.at[s, k], r_r.at[s, k], far[k], me_p
                    ))

    def gather(c):
        share(c)
        forward(c)

    if C == 4:
        gather(0)
        gather(1)
        forth(0)
        gather(2)
        forth(1)
        gather(3)
        forth(2)
        forth(3)
        back(2)
        back(0)
        z_step(2)
        back(3)
        z_step(0)
        back(1, lambda: z_step(3))
        z_step(1)
    else:
        for c in range(C):
            gather(c)
            forth(c)
            back(c)
            z_step(c)

    tn = (((0,), (0,)), ((), ()))
    ends = []
    for s, (lo, n) in enumerate(pieces):
        for k in range(1, NE):
            rets[k, s].wait_recv()
        here = pl.ds(lo, n)
        cols = aligned(my_base + lo, n)
        piece = ret[:, :, lo : lo + n].reshape(C * M, n)
        for j in order + [0]:
            pick = pm[:, :, aligned(peers[j] * T, T)].reshape(C * M, T)
            rows_j = lax.dot_general(pick, piece, tn, preferred_element_type=F32).astype(BF)
            if j:
                fs[j, :, here] = rows_j
                ends.append(go(remote(fs.at[j, :, here], out.at[:, cols], f_s.at[s, j], f_r.at[s, j], me_e, peers[j])))
            else:
                out[:, cols] = rows_j
    for copy in ends:
        copy.wait_recv()
    for copy in started:
        copy.wait_send()


def on_device(NE, NP, tokens, hidden_grad, routes, exponents, gate_weight, up_weight):
    T, D = tokens.shape
    FL = gate_weight.shape[2]
    group = NP * T
    experts = NE * gate_weight.shape[0]
    cap = -(-max(2, 5 * group // (4 * experts)) // 16) * 16
    C = min(4, NE)
    M = NE // C * cap
    Q, H = D // 4, D // 2
    V = pltpu.VMEM
    dma = pltpu.SemaphoreType.DMA
    return pl.pallas_call(
        functools.partial(kernel, NE, NP, C, cap),
        out_shape=jax.ShapeDtypeStruct((T, D), BF),
        in_specs=[pl.BlockSpec(memory_space=V)] * 2 + [pl.BlockSpec(memory_space=pl.ANY)] * 4,
        out_specs=pl.BlockSpec(memory_space=V),
        scratch_shapes=[
            V((NP, 1, T), jnp.int32),
            V((NP, 1, T), jnp.int32),
            V((NP, T, Q), BF),
            V((NP, T, FL), BF),
            V((C, M, group), BF),
            V((C, M, Q), BF),
            V((C, M, FL), BF),
            V((C, M, D), BF),
            V((C, M, FL), BF),
            V((D, FL), BF),
            V((D, FL), BF),
            V((FL, D), BF),
            V((FL, D), BF),
            V((C, M, FL), F32),
            V((C, M, FL), F32),
            V((M, FL), BF),
            V((M, FL), BF),
            V((C, M, H), BF),
            V((C, M, H), F32),
            V((C, M, H), BF),
            V((C, M, Q), BF),
            V((C, M, Q), BF),
            V((C, M, Q), BF),
            V((C, M, Q), BF),
            V((NP, T, Q), BF),
            dma((4,)),
            dma((NP,)), dma((NP,)), dma((NP,)), dma((NP,)),
            dma((2, NP)), dma((2, NP)), dma((NP,)), dma((NP,)),
            dma((2, NE)), dma((2, NE)), dma((NE,)), dma((NE,)),
            dma((3, C)), dma((3, C)),
            dma((2, C)), dma((2, C)), dma((2, C)), dma((2, C)),
            dma((2, NE)), dma((2, NE)),
            dma((2, NP)), dma((2, NP)),
        ],
        compiler_params=pltpu.CompilerParams(
            collective_id=0, has_side_effects=True, vmem_limit_bytes=60 * 1024 * 1024
        ),
    )(routes.reshape(1, T), exponents.reshape(1, T), tokens, hidden_grad, gate_weight, up_weight)


def solution(mesh):
    placed = (
        P(("expert", "etp"), None),
        P(("expert", "etp"), None),
        P(("expert", "etp"), None),
        P(("expert", "etp")),
        P("expert", None, "etp"),
        P("expert", None, "etp"),
    )
    body = functools.partial(on_device, mesh.shape["expert"], mesh.shape["etp"])
    return jax.shard_map(
        body, mesh=mesh, in_specs=placed, out_specs=P(("expert", "etp"), None), check_vma=False
    )
```
